32 devices in a mesh: job: 2 (over x), tm: 2 (over core), rows: 8 (over z, y).
Axes of the slice: x: 2, y: 2, z: 4, core: 2. Of those that a mesh axis runs over, the one named last changes fastest.
Arguments:
- prior: bfloat16 [2, 524288, 64], P('tm', ('job', 'rows')), parts along dimension 1, may hold values from -80 to 80
- snapshots: bfloat16 [2, 524288, 256], P('tm', ('job', 'rows')), parts along dimension 1, may hold values from -60 to 60
Outputs:
- merged: bfloat16 [524288, 64], P(('job', 'rows'), 'tm'), parts along dimension 0
The draws below stay inside these ranges and needn't reach their ends.
There are 2 independent parts, one for each index of `job`. The reference program is written for one: setup_inputs(seed, part) draws one part's arguments, and reference() takes and returns one part's arrays. A program takes and returns all parts, laid end to end along the dimension named above; each array names one. Nothing has to cross between parts.
All inputs are finite; a program needn't handle non-finite values.
Results may differ from the reference program's by a relative error of at most 0.011.
Values may be sent and summed in bfloat16 or wider, within the bound.
A program may use at most 128 MiB of HBM per device.

```python
import jax
import jax.numpy as jnp
from jax import lax

KEEP = 64
NEW = 64
STEPS = 4
ITERS = 2
DOFS = 262144
SNAPS = 256
N_TM = 2


def shared_fields(key):
    fields = 3 * KEEP + NEW
    key_u, key_r, key_s = jax.random.split(jax.random.fold_in(key, 5), 3)
    spatial = jnp.clip(jax.random.normal(key_u, (DOFS, fields), jnp.float32), -5.0, 5.0)
    row_scale = jnp.exp(jax.random.uniform(key_r, (DOFS, 1), jnp.float32, jnp.log(0.3), jnp.log(3.0)))
    ranks = jnp.arange(fields, dtype=jnp.float32)
    spectrum = 3.0 / (1.0 + ranks / 16.0)
    jitter = jnp.exp(jax.random.uniform(key_s, (fields,), jnp.float32, jnp.log(0.7), jnp.log(1.4)))
    return (spatial * row_scale * (spectrum * jitter)[None, :], row_scale)


def mixed_field(key, shape):
    return jnp.clip(jax.random.normal(key, shape, jnp.float32), -5.0, 5.0)


def draw_prior(key, part):
    scaled, row_scale = shared_fields(key)
    fields = scaled.shape[1]
    own = jax.random.fold_in(key, 11)
    key_m, key_n, key_c = jax.random.split(own, 3)
    mixing = mixed_field(key_m, (N_TM, fields, KEEP)) * 0.25
    col_scale = jnp.exp(jax.random.uniform(key_c, (N_TM, 1, KEEP), jnp.float32, jnp.log(0.5), jnp.log(2.0)))
    values = jnp.einsum('dr,trk->tdk', scaled, mixing, precision=jax.lax.Precision.HIGHEST)
    noise = 0.2 * mixed_field(key_n, (N_TM, DOFS, KEEP)) * row_scale[None]
    return jnp.clip((values + noise) * col_scale, -80.0, 80.0).astype(jnp.bfloat16)


def draw_snapshots(key, part):
    scaled, row_scale = shared_fields(key)
    fields = scaled.shape[1]
    own = jax.random.fold_in(key, 23)
    key_a, key_n, key_c = jax.random.split(own, 3)
    amplitude = mixed_field(key_a, (N_TM, fields, SNAPS)) * 0.3
    col_scale = jnp.exp(jax.random.uniform(key_c, (N_TM, 1, SNAPS), jnp.float32, jnp.log(0.5), jnp.log(2.0)))
    values = jnp.einsum('dr,trs->tds', scaled, amplitude, precision=jax.lax.Precision.HIGHEST)
    noise = 0.2 * mixed_field(key_n, (N_TM, DOFS, SNAPS)) * row_scale[None]
    values = values + noise
    return jnp.clip(values * col_scale, -60.0, 60.0).astype(jnp.bfloat16)


def setup_inputs(seed: int = 0, part: int = 0) -> dict:
    key_list = jax.random.split(jax.random.key(seed), 3)
    own_keys = jax.random.split(jax.random.fold_in(key_list[2], part), 3)
    return {
        "prior": draw_prior(jax.random.fold_in(jax.random.fold_in(key_list[2], part), 71), part),
        "snapshots": draw_snapshots(jax.random.fold_in(jax.random.fold_in(key_list[2], part), 71), part),
    }


def basis_of(gram, keep):
    order = gram.shape[0]
    basis = jnp.eye(order, keep, dtype=jnp.float32)
    for turn in range(ITERS):
        image = jnp.dot(gram, basis, precision=lax.Precision.HIGHEST)
        inner = jnp.dot(image.T, image, precision=lax.Precision.HIGHEST)
        lower = jnp.linalg.cholesky(inner)
        basis = jax.scipy.linalg.solve_triangular(lower, image.T, lower=True).T
    return basis

def reduce_pair(joined):
    gram = jnp.dot(joined.T, joined, precision=lax.Precision.HIGHEST)
    basis = basis_of(gram, KEEP)
    return jnp.dot(joined, basis, precision=lax.Precision.HIGHEST)

def reference(prior, snapshots):
    groups = []
    for group in range(N_TM):
        modes = prior[group].astype(jnp.float32)
        for step in range(STEPS):
            fresh = snapshots[group][:, step * NEW:(step + 1) * NEW].astype(jnp.float32)
            modes = reduce_pair(jnp.concatenate([modes, fresh], axis=1))
        groups.append(modes)
    while len(groups) > 1:
        groups = [reduce_pair(jnp.concatenate([groups[2 * pos], groups[2 * pos + 1]], axis=1)) for pos in range(len(groups) // 2)]
    return groups[0].astype(jnp.bfloat16)
```

```python
import functools

import jax
import jax.numpy as jnp
from jax import lax
from jax.experimental import pallas as pl
from jax.experimental.pallas import tpu as pltpu
from jax.sharding import PartitionSpec as P

STEPS = 4
ITERS = 2
LANES = 128
SUB = 8
F32 = jnp.float32
BF16 = jnp.bfloat16
HIGH = lax.Precision.HIGHEST
MESH = pl.DeviceIdType.MESH
NT = (((1,), (1,)), ((), ()))
TN = (((0,), (0,)), ((), ()))


def vmem():
    return pl.BlockSpec(memory_space=pltpu.VMEM)


def nt(a, b):
    return lax.dot_general(a, b, NT, precision=HIGH, preferred_element_type=F32)


def nn(a, b):
    return jnp.dot(a, b, precision=HIGH, preferred_element_type=F32)


def two_parts(x):
    hi = x.astype(BF16)
    lo = (x - hi.astype(F32)).astype(BF16)
    return jnp.concatenate([hi, lo], axis=0)


def orthonormal(inner, image, c_ref, y_ref):
    order, wide = image.shape
    blocks = order // SUB
    c_ref[:, 0:order] = inner
    c_ref[:, order:] = jnp.zeros((order, wide - order), F32)
    y_ref[...] = image
    row = lax.broadcasted_iota(jnp.int32, (SUB, wide), 0)

    @pl.loop(0, blocks)
    def panel(_):
        cs = [c_ref[q * SUB:(q + 1) * SUB, :] for q in range(blocks)]
        ys = [y_ref[q * SUB:(q + 1) * SUB, :] for q in range(blocks)]
        cols = [[jnp.broadcast_to(c[:, k:k + 1], (SUB, wide)) for c in cs] for k in range(SUB)]
        pivots = jnp.ones((SUB, wide), F32)
        for j in range(SUB):
            pivot = cols[j][0][j:j + 1]
            pivots = jnp.where(row == j, pivot, pivots)
            inverse = 1.0 / pivot
            y_row, c_row = ys[0][j:j + 1] * inverse, cs[0][j:j + 1] * inverse
            heads = [cols[k][0][j:j + 1] * inverse for k in range(SUB)]
            for q in range(blocks):
                factor = cols[j][q]
                if q == 0:
                    factor = jnp.where(row > j, factor, 0.0)
                ys[q] = ys[q] - factor * y_row
                cs[q] = cs[q] - factor * c_row
                for k in range(j + 1, SUB):
                    cols[k][q] = cols[k][q] - factor * heads[k]
        done = ys[0] * lax.rsqrt(pivots)
        cs = [pltpu.roll(c, wide - SUB, 1) for c in cs[1:]] + [jnp.zeros((SUB, wide), F32)]
        for q, (c, y) in enumerate(zip(cs, ys[1:] + [done])):
            c_ref[q * SUB:(q + 1) * SUB, :] = c
            y_ref[q * SUB:(q + 1) * SUB, :] = y


def basis_rows(gram_ref, q_ref, image_ref, c_ref, keep):
    image_ref[...] = gram_ref[:keep, :]

    @pl.loop(0, ITERS)
    def turn(_):
        image = image_ref[...]
        orthonormal(nt(image, image), image, c_ref, q_ref)
        image_ref[...] = nn(q_ref[...], gram_ref[...])

    return image_ref[...]


def gram_kernel(prior_ref, frames_ref, pp_ref, ps_ref, ss_ref):
    @pl.when(pl.program_id(0) == 0)
    def _():
        pp_ref[...] = jnp.zeros_like(pp_ref)
        ps_ref[...] = jnp.zeros_like(ps_ref)
        ss_ref[...] = jnp.zeros_like(ss_ref)

    prior, frames = prior_ref[...], frames_ref[...]
    pp_ref[...] += lax.dot_general(prior, prior, NT, preferred_element_type=F32)
    ps_ref[...] += jnp.dot(prior, frames, preferred_element_type=F32)
    ss_ref[...] += lax.dot_general(frames, frames, TN, preferred_element_type=F32)


def gram_of(prior, frames, tile):
    keep, rows = prior.shape
    wide = frames.shape[1]
    return pl.pallas_call(
        gram_kernel,
        grid=(rows // tile,),
        in_specs=[
            pl.BlockSpec((keep, tile), lambda i: (0, i)),
            pl.BlockSpec((tile, wide), lambda i: (i, 0)),
        ],
        out_specs=[
            pl.BlockSpec((keep, keep), lambda i: (0, 0)),
            pl.BlockSpec((keep, wide), lambda i: (0, 0)),
            pl.BlockSpec((wide, wide), lambda i: (0, 0)),
        ],
        out_shape=[
            jax.ShapeDtypeStruct((keep, keep), F32),
            jax.ShapeDtypeStruct((keep, wide), F32),
            jax.ShapeDtypeStruct((wide, wide), F32),
        ],
    )(prior, frames)


def meet(peers):
    barrier = pltpu.get_barrier_semaphore()
    for peer in peers:
        pl.semaphore_signal(barrier, inc=1, device_id=peer, device_id_type=MESH)
    pl.semaphore_wait(barrier, len(peers))


def sum_kernel(n, half, pp_ref, ps_ref, ss_ref, opp_ref, ops_ref, oss_ref, mine, got, full, s1, r1, s2, r2):
    me = lax.axis_index("rows")
    keep = pp_ref.shape[0]
    wide = ss_ref.shape[0]
    mine[...] = jnp.zeros_like(mine)
    mine[0:keep, 0:keep] = pp_ref[...]
    at = keep
    for c in range(wide // half):
        mine[at:at + keep, :] = ps_ref[:, c * half:(c + 1) * half]
        at += keep
    for a in range(wide // half):
        for b in range(a, wide // half):
            mine[at:at + half, :] = ss_ref[a * half:(a + 1) * half, b * half:(b + 1) * half]
            at += half
    peers = [{"rows": lax.rem(me + o, n)} for o in range(1, n)]
    meet(peers)
    piece = mine.shape[0] // n
    own = pl.ds(pl.multiple_of(me * piece, SUB), piece)
    first = []
    for o, peer in enumerate(peers):
        there = pl.ds(pl.multiple_of(peer["rows"] * piece, SUB), piece)
        copy = pltpu.make_async_remote_copy(
            src_ref=mine.at[there], dst_ref=got.at[o], send_sem=s1.at[o], recv_sem=r1.at[o],
            device_id=peer, device_id_type=MESH)
        copy.start()
        first.append(copy)
    total = mine[own, :]
    for o, copy in enumerate(first):
        copy.wait_recv()
        total = total + got[o]
    full[own, :] = total
    second = []
    for o, peer in enumerate(peers):
        copy = pltpu.make_async_remote_copy(
            src_ref=full.at[own], dst_ref=full.at[own], send_sem=s2.at[o], recv_sem=r2.at[o],
            device_id=peer, device_id_type=MESH)
        copy.start()
        second.append(copy)
    for copy in second:
        copy.wait_recv()
    opp_ref[...] = full[0:keep, 0:keep]
    at = keep
    for c in range(wide // half):
        ops_ref[:, c * half:(c + 1) * half] = full[at:at + keep, :]
        at += keep
    for a in range(wide // half):
        for b in range(a, wide // half):
            block = full[at:at + half, :]
            oss_ref[a * half:(a + 1) * half, b * half:(b + 1) * half] = block
            if b > a:
                oss_ref[b * half:(b + 1) * half, a * half:(a + 1) * half] = block.T
            at += half
    for copy in first + second:
        copy.wait_send()


def sum_over_rows(pp, ps, ss):
    n = lax.axis_size("rows")
    keep, wide = ps.shape
    parts = wide // LANES
    rows = keep + parts * keep + parts * (parts + 1) // 2 * LANES
    rows = pl.cdiv(rows, SUB * n) * SUB * n
    dma = pltpu.SemaphoreType.DMA((n - 1,))
    return pl.pallas_call(
        functools.partial(sum_kernel, n, LANES),
        out_shape=[jax.ShapeDtypeStruct(x.shape, F32) for x in (pp, ps, ss)],
        in_specs=[vmem()] * 3,
        out_specs=[vmem()] * 3,
        scratch_shapes=[
            pltpu.VMEM((rows, LANES), F32),
            pltpu.VMEM((n - 1, rows // n, LANES), F32),
            pltpu.VMEM((rows, LANES), F32),
            dma, dma, dma, dma,
        ],
        compiler_params=pltpu.CompilerParams(collective_id=0, has_side_effects=True),
    )(pp, ps, ss)


def steps_kernel(pp_ref, ps_ref, ss_ref, wf_ref, wp_ref, own_ref, gram, q, held, square, weights, cross, heads, corners):
    keep, wide = ps_ref.shape
    fresh = wide // STEPS
    gram[0:keep, 0:keep] = pp_ref[...]
    for k in range(STEPS):
        heads[k] = ps_ref[:, k * fresh:(k + 1) * fresh]
        corners[k] = ss_ref[k * fresh:(k + 1) * fresh, k * fresh:(k + 1) * fresh]
    cross[...] = ps_ref[...]
    span = weights.shape[1]
    lane = lax.broadcasted_iota(jnp.int32, (fresh, span), 1)
    row = lax.broadcasted_iota(jnp.int32, (fresh, span), 0)
    weights[...] = jnp.where(lane == row + wide, 1.0, 0.0)

    def step(k, carry):
        head = heads[k]
        gram[0:keep, keep:] = head
        gram[keep:, 0:keep] = head.T
        gram[keep:, keep:] = corners[k]
        image = basis_rows(gram, q, held, square, keep)
        basis = q[...]
        gram[0:keep, 0:keep] = nt(image, basis)
        fresh_rows = ss_ref[pl.ds(pl.multiple_of(k * fresh, fresh), fresh), :]
        following = nn(basis, jnp.concatenate([cross[...], fresh_rows], axis=0))
        cross[...] = following
        for m in range(STEPS):
            heads[m] = following[:, m * fresh:(m + 1) * fresh]
        place = jnp.where(lane == row + k * fresh, 1.0, 0.0)
        weights[...] = nn(basis, jnp.concatenate([weights[...], place], axis=0))
        return carry

    lax.fori_loop(0, STEPS, step, 0)
    wf_ref[...] = two_parts(weights[:, 0:wide])
    wp_ref[...] = two_parts(weights[:, wide:wide + keep])
    own_ref[...] = jnp.zeros_like(own_ref)
    own_ref[:, 0:keep] = gram[0:keep, 0:keep]


def steps_of(pp, ps, ss):
    keep, wide = ps.shape
    fresh = wide // STEPS
    span = pl.cdiv(wide + keep, LANES) * LANES
    return pl.pallas_call(
        steps_kernel,
        out_shape=[
            jax.ShapeDtypeStruct((2 * keep, wide), BF16),
            jax.ShapeDtypeStruct((2 * keep, keep), BF16),
            jax.ShapeDtypeStruct((keep, LANES), F32),
        ],
        in_specs=[vmem()] * 3,
        out_specs=[vmem()] * 3,
        scratch_shapes=[
            pltpu.VMEM((keep + fresh, keep + fresh), F32),
            pltpu.VMEM((keep, keep + fresh), F32),
            pltpu.VMEM((keep, keep + fresh), F32),
            pltpu.VMEM((keep, keep + fresh), F32),
            pltpu.VMEM((keep, span), F32),
            pltpu.VMEM((keep, wide), F32),
            pltpu.VMEM((STEPS, keep, fresh), F32),
            pltpu.VMEM((STEPS, fresh, fresh), F32),
        ],
    )(pp, ps, ss)


def modes_kernel(prior_ref, frames_ref, wf_ref, wp_ref, out_ref):
    keep = out_ref.shape[0]
    both = jnp.dot(wp_ref[...], prior_ref[...], preferred_element_type=F32)
    both += lax.dot_general(wf_ref[...], frames_ref[...], NT, preferred_element_type=F32)
    out_ref[...] = (both[:keep] + both[keep:]).astype(BF16)


def modes_of(prior, frames, wf, wp, tile):
    keep, rows = prior.shape
    wide = frames.shape[1]
    return pl.pallas_call(
        modes_kernel,
        grid=(rows // tile,),
        in_specs=[
            pl.BlockSpec((keep, tile), lambda i: (0, i)),
            pl.BlockSpec((tile, wide), lambda i: (i, 0)),
            pl.BlockSpec(wf.shape, lambda i: (0, 0)),
            pl.BlockSpec(wp.shape, lambda i: (0, 0)),
        ],
        out_specs=pl.BlockSpec((keep, tile), lambda i: (0, i)),
        out_shape=jax.ShapeDtypeStruct((keep, rows), BF16),
    )(prior, frames, wf, wp)


def cross_kernel(own_ref, other_ref, out_ref):
    @pl.when(pl.program_id(0) == 0)
    def _():
        out_ref[...] = jnp.zeros_like(out_ref)

    out_ref[...] += lax.dot_general(own_ref[...], other_ref[...], NT, preferred_element_type=F32)


def cross_of(own, other, tile):
    keep, rows = own.shape
    return pl.pallas_call(
        cross_kernel,
        grid=(rows // tile,),
        in_specs=[pl.BlockSpec((keep, tile), lambda i: (0, i))] * 2,
        out_specs=pl.BlockSpec((keep, keep), lambda i: (0, 0)),
        out_shape=jax.ShapeDtypeStruct((keep, keep), F32),
    )(own, other)


def pair_kernel(n, cross_ref, own_ref, cross_out, other_out, mine, got, s1, r1, s2, r2):
    me, group = lax.axis_index("rows"), lax.axis_index("tm")
    keep = cross_ref.shape[0]
    half = keep // 2
    mine[:, 0:keep] = cross_ref[0:half, :]
    mine[:, keep:2 * keep] = cross_ref[half:keep, :]
    peers = [{"rows": lax.rem(me + o, n)} for o in range(1, n)]
    twin = {"tm": 1 - group}
    meet(peers + [twin])
    swap = pltpu.make_async_remote_copy(
        src_ref=own_ref, dst_ref=other_out, send_sem=s2, recv_sem=r2, device_id=twin, device_id_type=MESH)
    copies = []
    for o, peer in enumerate(peers):
        copy = pltpu.make_async_remote_copy(
            src_ref=mine, dst_ref=got.at[o], send_sem=s1.at[o], recv_sem=r1.at[o],
            device_id=peer, device_id_type=MESH)
        copy.start()
        copies.append(copy)
    swap.start()
    total = mine[...]
    for o, copy in enumerate(copies):
        copy.wait_recv()
        total = total + got[o]
    cross_out[0:half, :] = total[:, 0:keep]
    cross_out[half:keep, :] = total[:, keep:2 * keep]
    swap.wait_recv()
    for copy in copies + [swap]:
        copy.wait_send()


def pair_sums(cross, own):
    n = lax.axis_size("rows")
    keep = cross.shape[0]
    dma = pltpu.SemaphoreType.DMA((n - 1,))
    return pl.pallas_call(
        functools.partial(pair_kernel, n),
        out_shape=[jax.ShapeDtypeStruct(x.shape, F32) for x in (cross, own)],
        in_specs=[vmem()] * 2,
        out_specs=[vmem()] * 2,
        scratch_shapes=[
            pltpu.VMEM((keep // 2, 2 * keep), F32),
            pltpu.VMEM((n - 1, keep // 2, 2 * keep), F32),
            dma, dma, pltpu.SemaphoreType.DMA, pltpu.SemaphoreType.DMA,
        ],
        compiler_params=pltpu.CompilerParams(collective_id=1, has_side_effects=True),
    )(cross, own)


def merge_kernel(cross_ref, own_ref, other_ref, mine_ref, theirs_ref, gram, q, held, square):
    keep = cross_ref.shape[0]
    half = keep // 2
    lead = lax.axis_index("tm") == 0
    cross = cross_ref[...]
    turned = cross.T
    own, other = own_ref[:, 0:keep], other_ref[:, 0:keep]
    gram[0:keep, 0:keep] = jnp.where(lead, own, other)
    gram[keep:, keep:] = jnp.where(lead, other, own)
    gram[0:keep, keep:] = jnp.where(lead, cross, turned)
    gram[keep:, 0:keep] = jnp.where(lead, turned, cross)
    basis_rows(gram, q, held, square, keep)
    part = jnp.where(lead, q[0:half, :], q[half:keep, :])
    mine_ref[...] = two_parts(jnp.where(lead, part[:, 0:keep], part[:, keep:]))
    theirs_ref[...] = two_parts(jnp.where(lead, part[:, keep:], part[:, 0:keep]))


def merge_basis(cross, own, other):
    keep = cross.shape[0]
    return pl.pallas_call(
        merge_kernel,
        out_shape=[jax.ShapeDtypeStruct((keep, keep), BF16)] * 2,
        in_specs=[vmem()] * 3,
        out_specs=[vmem()] * 2,
        scratch_shapes=[pltpu.VMEM((2 * keep, 2 * keep), F32), pltpu.VMEM((keep, 2 * keep), F32)]
        + [pltpu.VMEM((keep, 2 * keep), F32)] * 2,
    )(cross, own, other)


def merged_kernel(own_ref, other_ref, mine_ref, theirs_ref, out_ref):
    half = out_ref.shape[0]
    both = jnp.dot(mine_ref[...], own_ref[...], preferred_element_type=F32)
    both += jnp.dot(theirs_ref[...], other_ref[...], preferred_element_type=F32)
    out_ref[...] = (both[:half] + both[half:]).astype(BF16)


def merged_of(own, other, mine, theirs, tile):
    keep, rows = own.shape
    half = keep // 2
    return pl.pallas_call(
        merged_kernel,
        grid=(rows // tile,),
        in_specs=[pl.BlockSpec((keep, tile), lambda i: (0, i))] * 2
        + [pl.BlockSpec(mine.shape, lambda i: (0, 0))] * 2,
        out_specs=pl.BlockSpec((half, tile), lambda i: (0, i)),
        out_shape=jax.ShapeDtypeStruct((half, rows), BF16),
    )(own, other, mine, theirs)


def shards(prior, snapshots):
    prior, frames = prior[0].T, snapshots[0]
    rows = frames.shape[0]
    tile = 2048 if rows % 2048 == 0 else rows
    wide_tile = 4096 if rows % 4096 == 0 else rows
    pp, ps, ss = sum_over_rows(*gram_of(prior, frames, tile))
    wf, wp, own_gram = steps_of(pp, ps, ss)
    own = modes_of(prior, frames, wf, wp, tile)
    other = lax.ppermute(own, "tm", [(0, 1), (1, 0)])
    cross, other_gram = pair_sums(cross_of(own, other, wide_tile), own_gram)
    mine, theirs = merge_basis(cross, own_gram, other_gram)
    return merged_of(own, other, mine, theirs, wide_tile).T


def solution(mesh):
    in_specs = (P("tm", ("job", "rows"), None), P("tm", ("job", "rows"), None))
    out_specs = P(("job", "rows"), "tm")
    return jax.shard_map(shards, mesh=mesh, in_specs=in_specs, out_specs=out_specs, check_vma=False)
```

```python
import functools

import jax
import jax.numpy as jnp
from jax import lax
from jax.experimental import pallas as pl
from jax.experimental.pallas import tpu as pltpu
from jax.sharding import PartitionSpec as P

STEPS = 4
ITERS = 2
LANES = 128
SUB = 8
F32 = jnp.float32
BF16 = jnp.bfloat16
HIGH = lax.Precision.HIGHEST
MESH = pl.DeviceIdType.MESH
NT = (((1,), (1,)), ((), ()))
TN = (((0,), (0,)), ((), ()))


def vmem():
    return pl.BlockSpec(memory_space=pltpu.VMEM)


def nt(a, b):
    return lax.dot_general(a, b, NT, precision=HIGH, preferred_element_type=F32)


def nn(a, b):
    return jnp.dot(a, b, precision=HIGH, preferred_element_type=F32)


def two_parts(x):
    hi = x.astype(BF16)
    lo = (x - hi.astype(F32)).astype(BF16)
    return jnp.concatenate([hi, lo], axis=0)


def orthonormal(inner, image, c_ref, y_ref):
    order, wide = image.shape
    blocks = order // SUB
    c_ref[:, 0:order] = inner
    c_ref[:, order:] = jnp.zeros((order, wide - order), F32)
    y_ref[...] = image
    row = lax.broadcasted_iota(jnp.int32, (SUB, wide), 0)

    @pl.loop(0, blocks)
    def panel(_):
        cs = [c_ref[q * SUB:(q + 1) * SUB, :] for q in range(blocks)]
        ys = [y_ref[q * SUB:(q + 1) * SUB, :] for q in range(blocks)]
        cols = [[jnp.broadcast_to(c[:, k:k + 1], (SUB, wide)) for c in cs] for k in range(SUB)]
        pivots = jnp.ones((SUB, wide), F32)
        for j in range(SUB):
            pivot = cols[j][0][j:j + 1]
            pivots = jnp.where(row == j, pivot, pivots)
            inverse = 1.0 / pivot
            y_row, c_row = ys[0][j:j + 1] * inverse, cs[0][j:j + 1] * inverse
            heads = [cols[k][0][j:j + 1] * inverse for k in range(SUB)]
            for q in range(blocks):
                factor = cols[j][q]
                if q == 0:
                    factor = jnp.where(row > j, factor, 0.0)
                ys[q] = ys[q] - factor * y_row
                cs[q] = cs[q] - factor * c_row
                for k in range(j + 1, SUB):
                    cols[k][q] = cols[k][q] - factor * heads[k]
        done = ys[0] * lax.rsqrt(pivots)
        cs = [pltpu.roll(c, wide - SUB, 1) for c in cs[1:]] + [jnp.zeros((SUB, wide), F32)]
        for q, (c, y) in enumerate(zip(cs, ys[1:] + [done])):
            c_ref[q * SUB:(q + 1) * SUB, :] = c
            y_ref[q * SUB:(q + 1) * SUB, :] = y


def basis_rows(gram_ref, q_ref, image_ref, c_ref, keep):
    image_ref[...] = gram_ref[:keep, :]

    @pl.loop(0, ITERS)
    def turn(_):
        image = image_ref[...]
        orthonormal(nt(image, image), image, c_ref, q_ref)
        image_ref[...] = nn(q_ref[...], gram_ref[...])

    return image_ref[...]


def gram_kernel(prior_ref, frames_ref, pp_ref, ps_ref, ss_ref):
    @pl.when(pl.program_id(0) == 0)
    def _():
        pp_ref[...] = jnp.zeros_like(pp_ref)
        ps_ref[...] = jnp.zeros_like(ps_ref)
        ss_ref[...] = jnp.zeros_like(ss_ref)

    prior, frames = prior_ref[...], frames_ref[...]
    pp_ref[...] += lax.dot_general(prior, prior, NT, preferred_element_type=F32)
    ps_ref[...] += jnp.dot(prior, frames, preferred_element_type=F32)
    ss_ref[...] += lax.dot_general(frames, frames, TN, preferred_element_type=F32)


def gram_of(prior, frames, tile):
    keep, rows = prior.shape
    wide = frames.shape[1]
    return pl.pallas_call(
        gram_kernel,
        grid=(rows // tile,),
        in_specs=[
            pl.BlockSpec((keep, tile), lambda i: (0, i)),
            pl.BlockSpec((tile, wide), lambda i: (i, 0)),
        ],
        out_specs=[
            pl.BlockSpec((keep, keep), lambda i: (0, 0)),
            pl.BlockSpec((keep, wide), lambda i: (0, 0)),
            pl.BlockSpec((wide, wide), lambda i: (0, 0)),
        ],
        out_shape=[
            jax.ShapeDtypeStruct((keep, keep), F32),
            jax.ShapeDtypeStruct((keep, wide), F32),
            jax.ShapeDtypeStruct((wide, wide), F32),
        ],
    )(prior, frames)


def meet(peers):
    barrier = pltpu.get_barrier_semaphore()
    for peer in peers:
        pl.semaphore_signal(barrier, inc=1, device_id=peer, device_id_type=MESH)
    pl.semaphore_wait(barrier, len(peers))


def sum_kernel(n, half, pp_ref, ps_ref, ss_ref, opp_ref, ops_ref, oss_ref, mine, got, full, s1, r1, s2, r2):
    me = lax.axis_index("rows")
    keep = pp_ref.shape[0]
    wide = ss_ref.shape[0]
    mine[...] = jnp.zeros_like(mine)
    mine[0:keep, 0:keep] = pp_ref[...]
    at = keep
    for c in range(wide // half):
        mine[at:at + keep, :] = ps_ref[:, c * half:(c + 1) * half]
        at += keep
    for a in range(wide // half):
        for b in range(a, wide // half):
            mine[at:at + half, :] = ss_ref[a * half:(a + 1) * half, b * half:(b + 1) * half]
            at += half
    peers = [{"rows": lax.rem(me + o, n)} for o in range(1, n)]
    meet(peers)
    piece = mine.shape[0] // n
    own = pl.ds(pl.multiple_of(me * piece, SUB), piece)
    first = []
    for o, peer in enumerate(peers):
        there = pl.ds(pl.multiple_of(peer["rows"] * piece, SUB), piece)
        copy = pltpu.make_async_remote_copy(
            src_ref=mine.at[there], dst_ref=got.at[o], send_sem=s1.at[o], recv_sem=r1.at[o],
            device_id=peer, device_id_type=MESH)
        copy.start()
        first.append(copy)
    total = mine[own, :]
    for o, copy in enumerate(first):
        copy.wait_recv()
        total = total + got[o]
    full[own, :] = total
    second = []
    for o, peer in enumerate(peers):
        copy = pltpu.make_async_remote_copy(
            src_ref=full.at[own], dst_ref=full.at[own], send_sem=s2.at[o], recv_sem=r2.at[o],
            device_id=peer, device_id_type=MESH)
        copy.start()
        second.append(copy)
    for copy in second:
        copy.wait_recv()
    opp_ref[...] = full[0:keep, 0:keep]
    at = keep
    for c in range(wide // half):
        ops_ref[:, c * half:(c + 1) * half] = full[at:at + keep, :]
        at += keep
    for a in range(wide // half):
        for b in range(a, wide // half):
            block = full[at:at + half, :]
            oss_ref[a * half:(a + 1) * half, b * half:(b + 1) * half] = block
            if b > a:
                oss_ref[b * half:(b + 1) * half, a * half:(a + 1) * half] = block.T
            at += half
    for copy in first + second:
        copy.wait_send()


def sum_over_rows(pp, ps, ss):
    n = lax.axis_size("rows")
    keep, wide = ps.shape
    parts = wide // LANES
    rows = keep + parts * keep + parts * (parts + 1) // 2 * LANES
    rows = pl.cdiv(rows, SUB * n) * SUB * n
    dma = pltpu.SemaphoreType.DMA((n - 1,))
    return pl.pallas_call(
        functools.partial(sum_kernel, n, LANES),
        out_shape=[jax.ShapeDtypeStruct(x.shape, F32) for x in (pp, ps, ss)],
        in_specs=[vmem()] * 3,
        out_specs=[vmem()] * 3,
        scratch_shapes=[
            pltpu.VMEM((rows, LANES), F32),
            pltpu.VMEM((n - 1, rows // n, LANES), F32),
            pltpu.VMEM((rows, LANES), F32),
            dma, dma, dma, dma,
        ],
        compiler_params=pltpu.CompilerParams(collective_id=0, has_side_effects=True),
    )(pp, ps, ss)


def steps_kernel(pp_ref, ps_ref, ss_ref, wf_ref, wp_ref, own_ref, gram, q, held, square, weights, cross, heads, corners):
    keep, wide = ps_ref.shape
    fresh = wide // STEPS
    gram[0:keep, 0:keep] = pp_ref[...]
    for k in range(STEPS):
        heads[k] = ps_ref[:, k * fresh:(k + 1) * fresh]
        corners[k] = ss_ref[k * fresh:(k + 1) * fresh, k * fresh:(k + 1) * fresh]
    cross[...] = ps_ref[...]
    span = weights.shape[1]
    lane = lax.broadcasted_iota(jnp.int32, (fresh, span), 1)
    row = lax.broadcasted_iota(jnp.int32, (fresh, span), 0)
    weights[...] = jnp.where(lane == row + wide, 1.0, 0.0)

    def step(k, carry):
        head = heads[k]
        gram[0:keep, keep:] = head
        gram[keep:, 0:keep] = head.T
        gram[keep:, keep:] = corners[k]
        image = basis_rows(gram, q, held, square, keep)
        basis = q[...]
        gram[0:keep, 0:keep] = nt(image, basis)
        fresh_rows = ss_ref[pl.ds(pl.multiple_of(k * fresh, fresh), fresh), :]
        following = nn(basis, jnp.concatenate([cross[...], fresh_rows], axis=0))
        cross[...] = following
        for m in range(STEPS):
            heads[m] = following[:, m * fresh:(m + 1) * fresh]
        place = jnp.where(lane == row + k * fresh, 1.0, 0.0)
        weights[...] = nn(basis, jnp.concatenate([weights[...], place], axis=0))
        return carry

    lax.fori_loop(0, STEPS, step, 0)
    wf_ref[...] = two_parts(weights[:, 0:wide])
    wp_ref[...] = two_parts(weights[:, wide:wide + keep])
    own_ref[...] = jnp.zeros_like(own_ref)
    own_ref[:, 0:keep] = gram[0:keep, 0:keep]


def steps_of(pp, ps, ss):
    keep, wide = ps.shape
    fresh = wide // STEPS
    span = pl.cdiv(wide + keep, LANES) * LANES
    return pl.pallas_call(
        steps_kernel,
        out_shape=[
            jax.ShapeDtypeStruct((2 * keep, wide), BF16),
            jax.ShapeDtypeStruct((2 * keep, keep), BF16),
            jax.ShapeDtypeStruct((keep, LANES), F32),
        ],
        in_specs=[vmem()] * 3,
        out_specs=[vmem()] * 3,
        scratch_shapes=[
            pltpu.VMEM((keep + fresh, keep + fresh), F32),
            pltpu.VMEM((keep, keep + fresh), F32),
            pltpu.VMEM((keep, keep + fresh), F32),
            pltpu.VMEM((keep, keep + fresh), F32),
            pltpu.VMEM((keep, span), F32),
            pltpu.VMEM((keep, wide), F32),
            pltpu.VMEM((STEPS, keep, fresh), F32),
            pltpu.VMEM((STEPS, fresh, fresh), F32),
        ],
    )(pp, ps, ss)


def modes_kernel(prior_ref, frames_ref, wf_ref, wp_ref, out_ref):
    keep = out_ref.shape[0]
    both = jnp.dot(wp_ref[...], prior_ref[...], preferred_element_type=F32)
    both += lax.dot_general(wf_ref[...], frames_ref[...], NT, preferred_element_type=F32)
    out_ref[...] = (both[:keep] + both[keep:]).astype(BF16)


def modes_of(prior, frames, wf, wp, tile):
    keep, rows = prior.shape
    wide = frames.shape[1]
    return pl.pallas_call(
        modes_kernel,
        grid=(rows // tile,),
        in_specs=[
            pl.BlockSpec((keep, tile), lambda i: (0, i)),
            pl.BlockSpec((tile, wide), lambda i: (i, 0)),
            pl.BlockSpec(wf.shape, lambda i: (0, 0)),
            pl.BlockSpec(wp.shape, lambda i: (0, 0)),
        ],
        out_specs=pl.BlockSpec((keep, tile), lambda i: (0, i)),
        out_shape=jax.ShapeDtypeStruct((keep, rows), BF16),
    )(prior, frames, wf, wp)


def cross_kernel(own_ref, other_ref, out_ref):
    @pl.when(pl.program_id(0) == 0)
    def _():
        out_ref[...] = jnp.zeros_like(out_ref)

    out_ref[...] += lax.dot_general(own_ref[...], other_ref[...], NT, preferred_element_type=F32)


def cross_of(own, other, tile):
    keep, rows = own.shape
    return pl.pallas_call(
        cross_kernel,
        grid=(rows // tile,),
        in_specs=[pl.BlockSpec((keep, tile), lambda i: (0, i))] * 2,
        out_specs=pl.BlockSpec((keep, keep), lambda i: (0, 0)),
        out_shape=jax.ShapeDtypeStruct((keep, keep), F32),
    )(own, other)


def pair_kernel(n, cross_ref, own_ref, cross_out, other_out, mine, got, s1, r1, s2, r2):
    me, group = lax.axis_index("rows"), lax.axis_index("tm")
    keep = cross_ref.shape[0]
    half = keep // 2
    mine[:, 0:keep] = cross_ref[0:half, :]
    mine[:, keep:2 * keep] = cross_ref[half:keep, :]
    peers = [{"rows": lax.rem(me + o, n)} for o in range(1, n)]
    twin = {"tm": 1 - group}
    meet(peers + [twin])
    swap = pltpu.make_async_remote_copy(
        src_ref=own_ref, dst_ref=other_out, send_sem=s2, recv_sem=r2, device_id=twin, device_id_type=MESH)
    copies = []
    for o, peer in enumerate(peers):
        copy = pltpu.make_async_remote_copy(
            src_ref=mine, dst_ref=got.at[o], send_sem=s1.at[o], recv_sem=r1.at[o],
            device_id=peer, device_id_type=MESH)
        copy.start()
        copies.append(copy)
    swap.start()
    total = mine[...]
    for o, copy in enumerate(copies):
        copy.wait_recv()
        total = total + got[o]
    cross_out[0:half, :] = total[:, 0:keep]
    cross_out[half:keep, :] = total[:, keep:2 * keep]
    swap.wait_recv()
    for copy in copies + [swap]:
        copy.wait_send()


def pair_sums(cross, own):
    n = lax.axis_size("rows")
    keep = cross.shape[0]
    dma = pltpu.SemaphoreType.DMA((n - 1,))
    return pl.pallas_call(
        functools.partial(pair_kernel, n),
        out_shape=[jax.ShapeDtypeStruct(x.shape, F32) for x in (cross, own)],
        in_specs=[vmem()] * 2,
        out_specs=[vmem()] * 2,
        scratch_shapes=[
            pltpu.VMEM((keep // 2, 2 * keep), F32),
            pltpu.VMEM((n - 1, keep // 2, 2 * keep), F32),
            dma, dma, pltpu.SemaphoreType.DMA, pltpu.SemaphoreType.DMA,
        ],
        compiler_params=pltpu.CompilerParams(collective_id=1, has_side_effects=True),
    )(cross, own)


def merge_kernel(cross_ref, own_ref, other_ref, mine_ref, theirs_ref, gram, q, held, square):
    keep = cross_ref.shape[0]
    half = keep // 2
    lead = lax.axis_index("tm") == 0
    cross = cross_ref[...]
    turned = cross.T
    own, other = own_ref[:, 0:keep], other_ref[:, 0:keep]
    gram[0:keep, 0:keep] = jnp.where(lead, own, other)
    gram[keep:, keep:] = jnp.where(lead, other, own)
    gram[0:keep, keep:] = jnp.where(lead, cross, turned)
    gram[keep:, 0:keep] = jnp.where(lead, turned, cross)
    basis_rows(gram, q, held, square, keep)
    part = jnp.where(lead, q[0:half, :], q[half:keep, :])
    mine_ref[...] = two_parts(jnp.where(lead, part[:, 0:keep], part[:, keep:]))
    theirs_ref[...] = two_parts(jnp.where(lead, part[:, keep:], part[:, 0:keep]))


def merge_basis(cross, own, other):
    keep = cross.shape[0]
    return pl.pallas_call(
        merge_kernel,
        out_shape=[jax.ShapeDtypeStruct((keep, keep), BF16)] * 2,
        in_specs=[vmem()] * 3,
        out_specs=[vmem()] * 2,
        scratch_shapes=[pltpu.VMEM((2 * keep, 2 * keep), F32), pltpu.VMEM((keep, 2 * keep), F32)]
        + [pltpu.VMEM((keep, 2 * keep), F32)] * 2,
    )(cross, own, other)


def merged_kernel(own_ref, other_ref, mine_ref, theirs_ref, out_ref):
    half = out_ref.shape[0]
    both = jnp.dot(mine_ref[...], own_ref[...], preferred_element_type=F32)
    both += jnp.dot(theirs_ref[...], other_ref[...], preferred_element_type=F32)
    out_ref[...] = (both[:half] + both[half:]).astype(BF16)


def merged_of(own, other, mine, theirs, tile):
    keep, rows = own.shape
    half = keep // 2
    return pl.pallas_call(
        merged_kernel,
        grid=(rows // tile,),
        in_specs=[pl.BlockSpec((keep, tile), lambda i: (0, i))] * 2
        + [pl.BlockSpec(mine.shape, lambda i: (0, 0))] * 2,
        out_specs=pl.BlockSpec((half, tile), lambda i: (0, i)),
        out_shape=jax.ShapeDtypeStruct((half, rows), BF16),
    )(own, other, mine, theirs)


def shards(prior, snapshots):
    prior, frames = prior[0].T, snapshots[0]
    rows = frames.shape[0]
    tile = 4096 if rows % 4096 == 0 else rows
    wide_tile = 8192 if rows % 8192 == 0 else rows
    pp, ps, ss = sum_over_rows(*gram_of(prior, frames, tile))
    wf, wp, own_gram = steps_of(pp, ps, ss)
    own = modes_of(prior, frames, wf, wp, tile)
    other = lax.ppermute(own, "tm", [(0, 1), (1, 0)])
    cross, other_gram = pair_sums(cross_of(own, other, wide_tile), own_gram)
    mine, theirs = merge_basis(cross, own_gram, other_gram)
    return merged_of(own, other, mine, theirs, wide_tile).T


def solution(mesh):
    in_specs = (P("tm", ("job", "rows"), None), P("tm", ("job", "rows"), None))
    out_specs = P(("job", "rows"), "tm")
    return jax.shard_map(shards, mesh=mesh, in_specs=in_specs, out_specs=out_specs, check_vma=False)
```

```python
import functools

import jax
import jax.numpy as jnp
from jax import lax
from jax.experimental import pallas as pl
from jax.experimental.pallas import tpu as pltpu
from jax.sharding import PartitionSpec as P

STEPS = 4
ITERS = 2
LANES = 128
SUB = 8
F32 = jnp.float32
BF16 = jnp.bfloat16
HIGH = lax.Precision.HIGHEST
MESH = pl.DeviceIdType.MESH
NT = (((1,), (1,)), ((), ()))
TN = (((0,), (0,)), ((), ()))


def vmem():
    return pl.BlockSpec(memory_space=pltpu.VMEM)


def nt(a, b):
    return lax.dot_general(a, b, NT, precision=HIGH, preferred_element_type=F32)


def nn(a, b):
    return jnp.dot(a, b, precision=HIGH, preferred_element_type=F32)


def two_parts(x):
    hi = x.astype(BF16)
    lo = (x - hi.astype(F32)).astype(BF16)
    return jnp.concatenate([hi, lo], axis=0)


def orthonormal(inner, image, c_ref, y_ref):
    order, wide = image.shape
    blocks = order // SUB
    c_ref[:, 0:order] = inner
    c_ref[:, order:] = jnp.zeros((order, wide - order), F32)
    y_ref[...] = image
    row = lax.broadcasted_iota(jnp.int32, (SUB, wide), 0)

    @pl.loop(0, blocks)
    def panel(_):
        cs = [c_ref[q * SUB:(q + 1) * SUB, :] for q in range(blocks)]
        ys = [y_ref[q * SUB:(q + 1) * SUB, :] for q in range(blocks)]
        cols = [[jnp.broadcast_to(c[:, k:k + 1], (SUB, wide)) for c in cs] for k in range(SUB)]
        pivots = jnp.ones((SUB, wide), F32)
        for j in range(SUB):
            pivot = cols[j][0][j:j + 1]
            pivots = jnp.where(row == j, pivot, pivots)
            inverse = 1.0 / pivot
            y_row, c_row = ys[0][j:j + 1] * inverse, cs[0][j:j + 1] * inverse
            heads = [cols[k][0][j:j + 1] * inverse for k in range(SUB)]
            for q in range(blocks):
                factor = cols[j][q]
                if q == 0:
                    factor = jnp.where(row > j, factor, 0.0)
                ys[q] = ys[q] - factor * y_row
                cs[q] = cs[q] - factor * c_row
                for k in range(j + 1, SUB):
                    cols[k][q] = cols[k][q] - factor * heads[k]
        done = ys[0] * lax.rsqrt(pivots)
        cs = [pltpu.roll(c, wide - SUB, 1) for c in cs[1:]] + [jnp.zeros((SUB, wide), F32)]
        for q, (c, y) in enumerate(zip(cs, ys[1:] + [done])):
            c_ref[q * SUB:(q + 1) * SUB, :] = c
            y_ref[q * SUB:(q + 1) * SUB, :] = y


def basis_rows(gram_ref, q_ref, image_ref, c_ref, keep):
    image_ref[...] = gram_ref[:keep, :]

    @pl.loop(0, ITERS)
    def turn(_):
        image = image_ref[...]
        orthonormal(nt(image, image), image, c_ref, q_ref)
        image_ref[...] = nn(q_ref[...], gram_ref[...])

    return image_ref[...]


def gram_kernel(prior_ref, frames_ref, pp_ref, ps_ref, ss_ref):
    @pl.when(pl.program_id(0) == 0)
    def _():
        pp_ref[...] = jnp.zeros_like(pp_ref)
        ps_ref[...] = jnp.zeros_like(ps_ref)
        ss_ref[...] = jnp.zeros_like(ss_ref)

    prior, frames = prior_ref[...], frames_ref[...]
    pp_ref[...] += lax.dot_general(prior, prior, NT, preferred_element_type=F32)
    ps_ref[...] += jnp.dot(prior, frames, preferred_element_type=F32)
    ss_ref[...] += lax.dot_general(frames, frames, TN, preferred_element_type=F32)


def gram_of(prior, frames, tile):
    keep, rows = prior.shape
    wide = frames.shape[1]
    return pl.pallas_call(
        gram_kernel,
        grid=(rows // tile,),
        in_specs=[
            pl.BlockSpec((keep, tile), lambda i: (0, i)),
            pl.BlockSpec((tile, wide), lambda i: (i, 0)),
        ],
        out_specs=[
            pl.BlockSpec((keep, keep), lambda i: (0, 0)),
            pl.BlockSpec((keep, wide), lambda i: (0, 0)),
            pl.BlockSpec((wide, wide), lambda i: (0, 0)),
        ],
        out_shape=[
            jax.ShapeDtypeStruct((keep, keep), F32),
            jax.ShapeDtypeStruct((keep, wide), F32),
            jax.ShapeDtypeStruct((wide, wide), F32),
        ],
    )(prior, frames)


def meet(peers):
    barrier = pltpu.get_barrier_semaphore()
    for peer in peers:
        pl.semaphore_signal(barrier, inc=1, device_id=peer, device_id_type=MESH)
    pl.semaphore_wait(barrier, len(peers))


def sum_kernel(n, half, pp_ref, ps_ref, ss_ref, opp_ref, ops_ref, oss_ref, mine, got, full, s1, r1, s2, r2):
    me = lax.axis_index("rows")
    keep = pp_ref.shape[0]
    wide = ss_ref.shape[0]
    mine[...] = jnp.zeros_like(mine)
    mine[0:keep, 0:keep] = pp_ref[...]
    at = keep
    for c in range(wide // half):
        mine[at:at + keep, :] = ps_ref[:, c * half:(c + 1) * half]
        at += keep
    for a in range(wide // half):
        for b in range(a, wide // half):
            mine[at:at + half, :] = ss_ref[a * half:(a + 1) * half, b * half:(b + 1) * half]
            at += half
    peers = [{"rows": lax.rem(me + o, n)} for o in range(1, n)]
    meet(peers)
    piece = mine.shape[0] // n
    own = pl.ds(pl.multiple_of(me * piece, SUB), piece)
    first = []
    for o, peer in enumerate(peers):
        there = pl.ds(pl.multiple_of(peer["rows"] * piece, SUB), piece)
        copy = pltpu.make_async_remote_copy(
            src_ref=mine.at[there], dst_ref=got.at[o], send_sem=s1.at[o], recv_sem=r1.at[o],
            device_id=peer, device_id_type=MESH)
        copy.start()
        first.append(copy)
    total = mine[own, :]
    for o, copy in enumerate(first):
        copy.wait_recv()
        total = total + got[o]
    full[own, :] = total
    second = []
    for o, peer in enumerate(peers):
        copy = pltpu.make_async_remote_copy(
            src_ref=full.at[own], dst_ref=full.at[own], send_sem=s2.at[o], recv_sem=r2.at[o],
            device_id=peer, device_id_type=MESH)
        copy.start()
        second.append(copy)
    for copy in second:
        copy.wait_recv()
    opp_ref[...] = full[0:keep, 0:keep]
    at = keep
    for c in range(wide // half):
        ops_ref[:, c * half:(c + 1) * half] = full[at:at + keep, :]
        at += keep
    for a in range(wide // half):
        for b in range(a, wide // half):
            block = full[at:at + half, :]
            oss_ref[a * half:(a + 1) * half, b * half:(b + 1) * half] = block
            if b > a:
                oss_ref[b * half:(b + 1) * half, a * half:(a + 1) * half] = block.T
            at += half
    for copy in first + second:
        copy.wait_send()


def sum_over_rows(pp, ps, ss):
    n = lax.axis_size("rows")
    keep, wide = ps.shape
    parts = wide // LANES
    rows = keep + parts * keep + parts * (parts + 1) // 2 * LANES
    rows = pl.cdiv(rows, SUB * n) * SUB * n
    dma = pltpu.SemaphoreType.DMA((n - 1,))
    return pl.pallas_call(
        functools.partial(sum_kernel, n, LANES),
        out_shape=[jax.ShapeDtypeStruct(x.shape, F32) for x in (pp, ps, ss)],
        in_specs=[vmem()] * 3,
        out_specs=[vmem()] * 3,
        scratch_shapes=[
            pltpu.VMEM((rows, LANES), F32),
            pltpu.VMEM((n - 1, rows // n, LANES), F32),
            pltpu.VMEM((rows, LANES), F32),
            dma, dma, dma, dma,
        ],
        compiler_params=pltpu.CompilerParams(collective_id=0, has_side_effects=True),
    )(pp, ps, ss)


def steps_kernel(pp_ref, ps_ref, ss_ref, wf_ref, wp_ref, own_ref, gram, q, held, square, weights, cross, heads, corners):
    keep, wide = ps_ref.shape
    fresh = wide // STEPS
    gram[0:keep, 0:keep] = pp_ref[...]
    for k in range(STEPS):
        heads[k] = ps_ref[:, k * fresh:(k + 1) * fresh]
        corners[k] = ss_ref[k * fresh:(k + 1) * fresh, k * fresh:(k + 1) * fresh]
    cross[...] = ps_ref[...]
    span = weights.shape[1]
    lane = lax.broadcasted_iota(jnp.int32, (fresh, span), 1)
    row = lax.broadcasted_iota(jnp.int32, (fresh, span), 0)
    weights[...] = jnp.where(lane == row + wide, 1.0, 0.0)

    def step(k, carry):
        head = heads[k]
        gram[0:keep, keep:] = head
        gram[keep:, 0:keep] = head.T
        gram[keep:, keep:] = corners[k]
        image = basis_rows(gram, q, held, square, keep)
        basis = q[...]
        gram[0:keep, 0:keep] = nt(image, basis)
        fresh_rows = ss_ref[pl.ds(pl.multiple_of(k * fresh, fresh), fresh), :]
        following = nn(basis, jnp.concatenate([cross[...], fresh_rows], axis=0))
        cross[...] = following
        for m in range(STEPS):
            heads[m] = following[:, m * fresh:(m + 1) * fresh]
        place = jnp.where(lane == row + k * fresh, 1.0, 0.0)
        weights[...] = nn(basis, jnp.concatenate([weights[...], place], axis=0))
        return carry

    lax.fori_loop(0, STEPS, step, 0)
    wf_ref[...] = two_parts(weights[:, 0:wide])
    wp_ref[...] = two_parts(weights[:, wide:wide + keep])
    own_ref[...] = jnp.zeros_like(own_ref)
    own_ref[:, 0:keep] = gram[0:keep, 0:keep]


def steps_of(pp, ps, ss):
    keep, wide = ps.shape
    fresh = wide // STEPS
    span = pl.cdiv(wide + keep, LANES) * LANES
    return pl.pallas_call(
        steps_kernel,
        out_shape=[
            jax.ShapeDtypeStruct((2 * keep, wide), BF16),
            jax.ShapeDtypeStruct((2 * keep, keep), BF16),
            jax.ShapeDtypeStruct((keep, LANES), F32),
        ],
        in_specs=[vmem()] * 3,
        out_specs=[vmem()] * 3,
        scratch_shapes=[
            pltpu.VMEM((keep + fresh, keep + fresh), F32),
            pltpu.VMEM((keep, keep + fresh), F32),
            pltpu.VMEM((keep, keep + fresh), F32),
            pltpu.VMEM((keep, keep + fresh), F32),
            pltpu.VMEM((keep, span), F32),
            pltpu.VMEM((keep, wide), F32),
            pltpu.VMEM((STEPS, keep, fresh), F32),
            pltpu.VMEM((STEPS, fresh, fresh), F32),
        ],
    )(pp, ps, ss)


def modes_kernel(prior_ref, frames_ref, wf_ref, wp_ref, out_ref):
    keep = out_ref.shape[0]
    both = jnp.dot(wp_ref[...], prior_ref[...], preferred_element_type=F32)
    both += lax.dot_general(wf_ref[...], frames_ref[...], NT, preferred_element_type=F32)
    out_ref[...] = (both[:keep] + both[keep:]).astype(BF16)


def modes_of(prior, frames, wf, wp, tile):
    keep, rows = prior.shape
    wide = frames.shape[1]
    return pl.pallas_call(
        modes_kernel,
        grid=(rows // tile,),
        in_specs=[
            pl.BlockSpec((keep, tile), lambda i: (0, i)),
            pl.BlockSpec((tile, wide), lambda i: (i, 0)),
            pl.BlockSpec(wf.shape, lambda i: (0, 0)),
            pl.BlockSpec(wp.shape, lambda i: (0, 0)),
        ],
        out_specs=pl.BlockSpec((keep, tile), lambda i: (0, i)),
        out_shape=jax.ShapeDtypeStruct((keep, rows), BF16),
    )(prior, frames, wf, wp)


def cross_kernel(own_ref, other_ref, out_ref):
    @pl.when(pl.program_id(0) == 0)
    def _():
        out_ref[...] = jnp.zeros_like(out_ref)

    out_ref[...] += lax.dot_general(own_ref[...], other_ref[...], NT, preferred_element_type=F32)


def cross_of(own, other, tile):
    keep, rows = own.shape
    return pl.pallas_call(
        cross_kernel,
        grid=(rows // tile,),
        in_specs=[pl.BlockSpec((keep, tile), lambda i: (0, i))] * 2,
        out_specs=pl.BlockSpec((keep, keep), lambda i: (0, 0)),
        out_shape=jax.ShapeDtypeStruct((keep, keep), F32),
    )(own, other)


def pair_kernel(n, cross_ref, own_ref, cross_out, other_out, mine, got, s1, r1, s2, r2):
    me, group = lax.axis_index("rows"), lax.axis_index("tm")
    keep = cross_ref.shape[0]
    half = keep // 2
    mine[:, 0:keep] = cross_ref[0:half, :]
    mine[:, keep:2 * keep] = cross_ref[half:keep, :]
    peers = [{"rows": lax.rem(me + o, n)} for o in range(1, n)]
    twin = {"tm": 1 - group}
    meet(peers + [twin])
    swap = pltpu.make_async_remote_copy(
        src_ref=own_ref, dst_ref=other_out, send_sem=s2, recv_sem=r2, device_id=twin, device_id_type=MESH)
    copies = []
    for o, peer in enumerate(peers):
        copy = pltpu.make_async_remote_copy(
            src_ref=mine, dst_ref=got.at[o], send_sem=s1.at[o], recv_sem=r1.at[o],
            device_id=peer, device_id_type=MESH)
        copy.start()
        copies.append(copy)
    swap.start()
    total = mine[...]
    for o, copy in enumerate(copies):
        copy.wait_recv()
        total = total + got[o]
    cross_out[0:half, :] = total[:, 0:keep]
    cross_out[half:keep, :] = total[:, keep:2 * keep]
    swap.wait_recv()
    for copy in copies + [swap]:
        copy.wait_send()


def pair_sums(cross, own):
    n = lax.axis_size("rows")
    keep = cross.shape[0]
    dma = pltpu.SemaphoreType.DMA((n - 1,))
    return pl.pallas_call(
        functools.partial(pair_kernel, n),
        out_shape=[jax.ShapeDtypeStruct(x.shape, F32) for x in (cross, own)],
        in_specs=[vmem()] * 2,
        out_specs=[vmem()] * 2,
        scratch_shapes=[
            pltpu.VMEM((keep // 2, 2 * keep), F32),
            pltpu.VMEM((n - 1, keep // 2, 2 * keep), F32),
            dma, dma, pltpu.SemaphoreType.DMA, pltpu.SemaphoreType.DMA,
        ],
        compiler_params=pltpu.CompilerParams(collective_id=1, has_side_effects=True),
    )(cross, own)


def merge_kernel(cross_ref, own_ref, other_ref, mine_ref, theirs_ref, gram, q, held, square):
    keep = cross_ref.shape[0]
    half = keep // 2
    lead = lax.axis_index("tm") == 0
    cross = cross_ref[...]
    turned = cross.T
    own, other = own_ref[:, 0:keep], other_ref[:, 0:keep]
    gram[0:keep, 0:keep] = jnp.where(lead, own, other)
    gram[keep:, keep:] = jnp.where(lead, other, own)
    gram[0:keep, keep:] = jnp.where(lead, cross, turned)
    gram[keep:, 0:keep] = jnp.where(lead, turned, cross)
    basis_rows(gram, q, held, square, keep)
    part = jnp.where(lead, q[0:half, :], q[half:keep, :])
    mine_ref[...] = two_parts(jnp.where(lead, part[:, 0:keep], part[:, keep:]))
    theirs_ref[...] = two_parts(jnp.where(lead, part[:, keep:], part[:, 0:keep]))


def merge_basis(cross, own, other):
    keep = cross.shape[0]
    return pl.pallas_call(
        merge_kernel,
        out_shape=[jax.ShapeDtypeStruct((keep, keep), BF16)] * 2,
        in_specs=[vmem()] * 3,
        out_specs=[vmem()] * 2,
        scratch_shapes=[pltpu.VMEM((2 * keep, 2 * keep), F32), pltpu.VMEM((keep, 2 * keep), F32)]
        + [pltpu.VMEM((keep, 2 * keep), F32)] * 2,
    )(cross, own, other)


def merged_kernel(own_ref, other_ref, mine_ref, theirs_ref, out_ref):
    half = out_ref.shape[0]
    both = jnp.dot(mine_ref[...], own_ref[...], preferred_element_type=F32)
    both += jnp.dot(theirs_ref[...], other_ref[...], preferred_element_type=F32)
    out_ref[...] = (both[:half] + both[half:]).astype(BF16)


def merged_of(own, other, mine, theirs, tile):
    keep, rows = own.shape
    half = keep // 2
    return pl.pallas_call(
        merged_kernel,
        grid=(rows // tile,),
        in_specs=[pl.BlockSpec((keep, tile), lambda i: (0, i))] * 2
        + [pl.BlockSpec(mine.shape, lambda i: (0, 0))] * 2,
        out_specs=pl.BlockSpec((half, tile), lambda i: (0, i)),
        out_shape=jax.ShapeDtypeStruct((half, rows), BF16),
    )(own, other, mine, theirs)


def shards(prior, snapshots):
    prior, frames = prior[0].T, snapshots[0]
    rows = frames.shape[0]
    tile = 8192 if rows % 8192 == 0 else rows
    wide_tile = 16384 if rows % 16384 == 0 else rows
    pp, ps, ss = sum_over_rows(*gram_of(prior, frames, tile))
    wf, wp, own_gram = steps_of(pp, ps, ss)
    own = modes_of(prior, frames, wf, wp, tile)
    other = lax.ppermute(own, "tm", [(0, 1), (1, 0)])
    cross, other_gram = pair_sums(cross_of(own, other, wide_tile), own_gram)
    mine, theirs = merge_basis(cross, own_gram, other_gram)
    return merged_of(own, other, mine, theirs, wide_tile).T


def solution(mesh):
    in_specs = (P("tm", ("job", "rows"), None), P("tm", ("job", "rows"), None))
    out_specs = P(("job", "rows"), "tm")
    return jax.shard_map(shards, mesh=mesh, in_specs=in_specs, out_specs=out_specs, check_vma=False)
```
